128 devices in a mesh: seq: 32 (over x_lo, z, y), head: 4 (over x_hi, core).
Axes of the slice: x: 4 (x_hi: 2, x_lo: 2; x = x_hi * 2 + x_lo), y: 4, z: 4, core: 2. Of those that a mesh axis runs over, the one named last changes fastest.
Arguments:
- queries: bfloat16 [16384, 5120], P('seq', 'head'), may hold values from -6 to 6
- keys: bfloat16 [16384, 5120], P('seq', 'head'), may hold values from -6 to 6
- values: bfloat16 [16384, 5120], P('seq', 'head'), may hold values from -6 to 6
- token_rate: float32 [16384, 8], P('seq', 'head'), may hold values from 0.1 to 1
- head_rate: float32 [8], P('head'), may hold values from 0.2 to 1
- fast_weights: bfloat16 [8, 3, 640, 640], P('head'), may hold values from -0.25 to 0.25
- ttt_gain: float32 [5120], P('head'), may hold values from 0.5 to 1.5
- out_weight: bfloat16 [5120, 5120], P('head', 'seq'), may hold values from -0.078125 to 0.078125
Outputs:
- mixed: bfloat16 [16384, 5120], P('seq', 'head')
The draws below stay inside these ranges and needn't reach their ends.
All inputs are finite; a program needn't handle non-finite values.
Results may differ from the reference program's by a relative error of at most 0.03.
Values may be sent and summed in bfloat16 or wider, within the bound.
No kernel may reach another device: no remote copies, remote signals or barrier semaphores. Data moves between devices by JAX's collectives and lax.ppermute only.
A program may use at most 128 MiB of HBM per device.

```python
import math
import jax
import jax.numpy as jnp
from jax import lax

HEADS = 8
HD = 640
AHD = 128
D = 5120
WINDOW = 1024
TOKENS = 16384
N_HEAD = 4


def draw_queries(key, part):
    field = jnp.clip(jax.random.normal(jax.random.fold_in(key, 1), (TOKENS, D), jnp.float32), -6.0, 6.0)
    return field.astype(jnp.bfloat16)


def draw_keys(key, part):
    field = jnp.clip(jax.random.normal(jax.random.fold_in(key, 2), (TOKENS, D), jnp.float32), -6.0, 6.0)
    return field.astype(jnp.bfloat16)


def level_of(key, dims, cuts, least, high):
    level = 1.0
    for position, shards_of in cuts:
        draws = jax.random.uniform(jax.random.fold_in(jax.random.fold_in(key, 6), position), (shards_of,), jnp.float32, least / len(cuts), high / len(cuts))
        level = level * jnp.repeat(jnp.exp(draws), dims[position] // shards_of).reshape((-1,) + (1,) * (len(dims) - 1 - position))
    return level


def scatter_about(own_key, dims, scale, bound, cuts=(), kind=jnp.bfloat16):
    entries = jax.random.normal(own_key, dims, jnp.float32) * scale
    if len(cuts) > 0:
        entries = level_of(own_key, dims, cuts, -0.22, 0.18) * entries
    return jnp.clip(entries, min=-bound, max=bound).astype(kind)


def setup_inputs(seed: int = 0) -> dict:
    arg_keys = jax.random.split(jax.random.key(seed), 9)
    queries = draw_queries(jax.random.fold_in(arg_keys[8], 71), 0)
    keys = draw_keys(jax.random.fold_in(arg_keys[8], 71), 0)
    values = scatter_about(arg_keys[2], (TOKENS, D), 1.0, 6.0, ((0, 32), (1, 4)))
    token_rate = jnp.clip(jnp.exp(math.log(1.0) - 2.3025851 * jax.random.uniform(arg_keys[3], (TOKENS, HEADS), jnp.float32) ** level_of(arg_keys[3], (TOKENS, HEADS), ((0, 32), (1, 4)), -0.2, 0.2)), 0.1, 1.0)
    head_rate = jnp.clip(jnp.exp(math.log(1.0) - 1.609438 * jax.random.uniform(arg_keys[4], (HEADS,), jnp.float32) ** level_of(arg_keys[4], (HEADS,), ((0, 4),), -0.2, 0.2)), 0.2, 1.0)
    fast_weights = scatter_about(arg_keys[5], (HEADS, 3, HD, HD), HD ** -0.5, 0.25, ((0, 4),))
    ttt_gain = jnp.clip(1.0 + 0.1 * jax.random.normal(arg_keys[6], (D,), jnp.float32), 0.5, 1.5)
    out_weight = scatter_about(arg_keys[7], (D, D), D ** -0.5, 0.078125, ((0, 4), (1, 32)))
    return dict(queries=queries, keys=keys, values=values, token_rate=token_rate, head_rate=head_rate, fast_weights=fast_weights, ttt_gain=ttt_gain, out_weight=out_weight)


EPS = 1e-06

def silu_slope(x):
    s = jax.nn.sigmoid(x)
    return s * (1.0 + x * (1.0 - s))

def renew(weight, descent, rate):
    mean_w = lax.optimization_barrier(jnp.mean(weight * weight, axis=(1, 2)))
    mean_d = lax.optimization_barrier(jnp.mean(descent * descent, axis=(1, 2)))
    factor = rate * jnp.sqrt((mean_w + EPS) / (mean_d + EPS))
    moved = weight + factor[:, None, None] * descent
    col_w = lax.optimization_barrier(jnp.mean(weight * weight, axis=1))
    col_m = lax.optimization_barrier(jnp.mean(moved * moved, axis=1))
    return (moved * jnp.sqrt((col_w + EPS) / (col_m + EPS))[:, None, :]).astype(jnp.bfloat16)

def fast_head(args):
    q_h, k_h, v_h, rate_h, w_h, hrate = args
    f32 = jnp.float32
    key_gate = jnp.dot(k_h, w_h[0], preferred_element_type=f32)
    key_up = jnp.dot(k_h, w_h[1], preferred_element_type=f32)
    key_act = (jax.nn.silu(key_gate) * key_up).astype(jnp.bfloat16)
    target = (rate_h[:, None] * v_h.astype(f32)).astype(jnp.bfloat16)
    back = jnp.dot(target, w_h[2].T, preferred_element_type=f32)
    grad_gate = (back * key_up * silu_slope(key_gate)).astype(jnp.bfloat16)
    grad_up = (back * jax.nn.silu(key_gate)).astype(jnp.bfloat16)
    desc = jnp.stack([jnp.dot(k_h.T, grad_gate, preferred_element_type=f32), jnp.dot(k_h.T, grad_up, preferred_element_type=f32), jnp.dot(key_act.T, target, preferred_element_type=f32)])
    updated = renew(w_h.astype(f32), desc, hrate)
    query_gate = jnp.dot(q_h, updated[0], preferred_element_type=f32)
    query_up = jnp.dot(q_h, updated[1], preferred_element_type=f32)
    query_act = (jax.nn.silu(query_gate) * query_up).astype(jnp.bfloat16)
    fast_out = jnp.dot(query_act, updated[2], preferred_element_type=f32)
    return fast_out * lax.rsqrt(lax.optimization_barrier(jnp.mean(fast_out * fast_out, axis=-1, keepdims=True)) + EPS)

def window_attention(queries, keys, values):
    heads_all = D // AHD
    padded_k = jnp.pad(keys, ((WINDOW, 0), (0, 0)))
    padded_v = jnp.pad(values, ((WINDOW, 0), (0, 0)))
    rows = jnp.arange(WINDOW, dtype=jnp.int32)[:, None] + WINDOW
    cols = jnp.arange(2 * WINDOW, dtype=jnp.int32)[None, :]

    def block(index):
        start = (index * WINDOW).astype(jnp.int32)
        qb = lax.dynamic_slice_in_dim(queries, start, WINDOW, 0).reshape(WINDOW, heads_all, AHD).astype(jnp.float32)
        kb = lax.dynamic_slice_in_dim(padded_k, start, 2 * WINDOW, 0).reshape(2 * WINDOW, heads_all, AHD).astype(jnp.float32)
        vb = lax.dynamic_slice_in_dim(padded_v, start, 2 * WINDOW, 0).reshape(2 * WINDOW, heads_all, AHD).astype(jnp.float32)
        scores = jnp.einsum('qhd,khd->hqk', qb, kb) / jnp.sqrt(jnp.float32(AHD))
        keep = (cols <= rows) & (cols > rows - WINDOW) & (cols + start >= WINDOW)
        scores = jnp.where(keep[None], scores, jnp.float32(-1e+30))
        top = lax.optimization_barrier(jnp.max(scores, axis=-1, keepdims=True))
        weights = jnp.exp(scores - top)
        probs = (weights / lax.optimization_barrier(jnp.sum(weights, axis=-1, keepdims=True))).astype(jnp.bfloat16)
        out = jnp.einsum('hqk,khd->qhd', probs.astype(jnp.float32), vb)
        return out.reshape(WINDOW, D)
    blocks = lax.map(block, jnp.arange(TOKENS // WINDOW, dtype=jnp.int32))
    return blocks.reshape(TOKENS, D)

def reference(queries, keys, values, token_rate, head_rate, fast_weights, ttt_gain, out_weight):

    def split(a):
        return a.reshape(TOKENS, HEADS, HD).transpose(1, 0, 2)
    fast = lax.map(fast_head, (split(queries), split(keys), split(values), token_rate.T, fast_weights, head_rate))
    fast_norm = fast.transpose(1, 0, 2).reshape(TOKENS, D) * ttt_gain[None, :]
    attn_out = window_attention(queries, keys, values)
    features = (fast_norm + attn_out).astype(jnp.bfloat16)
    group = D // N_HEAD
    total = jnp.zeros((TOKENS, D), jnp.float32)
    for index in range(N_HEAD):
        part = jnp.dot(features[:, index * group:(index + 1) * group], out_weight[index * group:(index + 1) * group], preferred_element_type=jnp.float32)
        part = lax.optimization_barrier(part.astype(jnp.bfloat16))
        total = total + part.astype(jnp.float32)
    return total.astype(jnp.bfloat16)
```

```python
import functools

import jax
import jax.numpy as jnp
from jax import lax
from jax.experimental import pallas as pl
from jax.experimental.pallas import tpu as pltpu
from jax.sharding import Mesh, PartitionSpec as P

AHD = 128
EPS = 1e-06
f32 = jnp.float32
bf16 = jnp.bfloat16


def hop(block, axis, distance):
    n = lax.axis_size(axis)
    return lax.ppermute(block, axis, [(i, (i + distance) % n) for i in range(n)])


def along_x(block, route):
    place = (0, 2, 1, 3)
    return lax.ppermute(block, ("xl", "xh"), [(place[a], place[b]) for a, b in route])


def next_ring(block, distance):
    axes = ("xl", "z", "y")
    route = [(i, i + 4) for i in range(28) if (i - distance) % 4 >= 2]
    return lax.ppermute(block, axes, route)


def dot(a, b, ca, cb):
    return lax.dot_general(a, b, (((ca,), (cb,)), ((), ())), preferred_element_type=f32)


def descent_kernel(at_ref, k_ref, t_ref, w_ref, *refs):
    k, target = k_ref[...], t_ref[...]
    gate = dot(k, w_ref[0, 0], 1, 0)
    up = dot(k, w_ref[0, 1], 1, 0)
    back = dot(target, w_ref[0, 2], 1, 1)
    s = jax.nn.sigmoid(gate)
    silu = gate * s
    act = (silu * up).astype(bf16)
    grad_gate = (back * up * (s * (1.0 + gate * (1.0 - s)))).astype(bf16)
    grad_up = (back * silu).astype(bf16)
    pairs = ((k, grad_gate), (k, grad_up), (act, target))
    if len(refs) == 1:
        for m, (a, b) in enumerate(pairs):
            refs[0][m] = dot(a, b, 0, 0)
        return
    sofar, out_ref = refs
    z, y = at_ref[1], at_ref[2]
    part = out_ref.shape[3]
    for m, (a, b) in enumerate(pairs):
        d = dot(a, b, 0, 0) + sofar[m]
        for i in range(4):
            for j in range(4):
                row = (4 * i + j) * part
                out_ref[lax.rem(i - z + 4, 4), lax.rem(j - y + 4, 4), m] = d[row : row + part].astype(bf16)


def descent_of(at, k, t, weights, sofar=None):
    rows, width = t.shape[0], weights.shape[2]
    own = k.shape[1] != width
    whole = lambda shape: pl.BlockSpec(shape, lambda i, at: (0,) * len(shape))
    specs = [
        pl.BlockSpec((rows, width), (lambda i, at: (0, at[0])) if own else (lambda i, at: (0, 0))),
        whole((rows, width)),
        pl.BlockSpec((1, 3, width, width), lambda i, at: (at[0], 0, 0, 0)),
    ]
    args = [k, t, weights]
    if sofar is None:
        shapes = [jax.ShapeDtypeStruct((3, width, width), f32)]
    else:
        specs.append(whole(sofar.shape))
        args.append(sofar)
        shapes = [jax.ShapeDtypeStruct((4, 4, 3, width // 16, width), bf16)]
    outs = pl.pallas_call(
        descent_kernel,
        out_shape=shapes,
        grid_spec=pltpu.PrefetchScalarGridSpec(
            num_scalar_prefetch=1, grid=(1,), in_specs=specs, out_specs=[whole(s.shape) for s in shapes]
        ),
        compiler_params=pltpu.CompilerParams(vmem_limit_bytes=56 << 20),
        cost_estimate=pl.CostEstimate(
            flops=12 * rows * width * width, bytes_accessed=10 << 20, transcendentals=rows * width
        ),
        name="descent" if sofar is None else "descent_got",
    )(at, *args)
    return outs[0]


def start_of(d):
    return 2 * d + jnp.where(d >= 2, 1, 0)


def pack_kernel(at_ref, *refs):
    ins, outs = refs[:12], refs[12:]
    for k in range(4):
        for i in range(3):
            outs[k][i, 0] = ins[3 * k + i][...]


def pack(at, queries, keys, values):
    rows = queries.shape[0]

    def spec(k):
        return pl.BlockSpec((rows, AHD), lambda s, at: (0, start_of(lax.rem(at[2] + k, 4)) + s))

    out = pl.BlockSpec((3, 1, rows, AHD), lambda s, at: (0, s, 0, 0))
    return pl.pallas_call(
        pack_kernel,
        out_shape=[jax.ShapeDtypeStruct((3, 3, rows, AHD), bf16)] * 4,
        grid_spec=pltpu.PrefetchScalarGridSpec(
            num_scalar_prefetch=1,
            grid=(3,),
            in_specs=[spec(k) for k in range(4) for _ in range(3)],
            out_specs=[out] * 4,
        ),
        cost_estimate=pl.CostEstimate(flops=0, bytes_accessed=10 << 20, transcendentals=0),
        name="pack",
    )(at, *[queries, keys, values] * 4)


def attend_kernel(tile, at_ref, g0, g1, g2, g3, h0, h1, h2, h3, out_ref, q_ref, kv_ref, sems):
    xl, z, y = at_ref[0], at_ref[1], at_ref[2]
    slot, yb = pl.program_id(0), pl.program_id(1)
    rows = q_ref.shape[2]

    def copies(act):
        for k in range(4):
            at = lax.rem(y - k + 4, 4)
            g, h = (g0, g1, g2, g3)[k], (h0, h1, h2, h3)[k]
            act(pltpu.make_async_copy(g.at[0], q_ref.at[at], sems.at[0, k]))
            act(pltpu.make_async_copy(g.at[pl.ds(1, 2)], kv_ref.at[at + 2], sems.at[1, k]))

            @pl.when(at >= 2)
            def _():
                act(pltpu.make_async_copy(h, kv_ref.at[at - 2], sems.at[2, k]))

    @pl.when((slot == 0) & (yb == 0))
    def _():
        copies(lambda c: c.start())
        copies(lambda c: c.wait())

    neg = f32(-1e30)
    first = (xl == 0) & (z == 0)
    bias1 = jnp.where(first & (yb < 1), neg, f32(0))
    bias2 = jnp.where(first & (yb < 2), neg, f32(0))
    scale = f32(1.0) / jnp.sqrt(f32(AHD))
    row = lax.broadcasted_iota(jnp.int32, (tile, tile), 0)
    col = lax.broadcasted_iota(jnp.int32, (tile, tile), 1)
    own = col <= row
    odd = lax.rem(y, 2)
    shared = slot == 2 - 2 * odd
    for t in range(rows // tile):

        @pl.when(jnp.logical_not(shared) | (odd == t))
        def _():
            lo, hi = t * tile, (t + 1) * tile
            q = q_ref[yb, slot, lo:hi, :]

            def score(d, a, b):
                return dot(q, kv_ref[yb + 2 - d, 0, slot, a:b, :], 1, 1) * scale

            def weigh(p, d, a, b):
                return dot(p.astype(bf16), kv_ref[yb + 2 - d, 1, slot, a:b, :], 1, 0)

            mix = jnp.where(own, score(0, lo, hi), score(2, lo, hi) + bias2)
            parts = [(score(1, 0, rows) + bias1, 1, 0, rows)]
            if lo > 0:
                parts.append((score(0, 0, lo), 0, 0, lo))
            if hi < rows:
                parts.append((score(2, hi, rows) + bias2, 2, hi, rows))
            top = jnp.max(mix, axis=1, keepdims=True)
            for s, _, _, _ in parts:
                top = jnp.maximum(top, jnp.max(s, axis=1, keepdims=True))
            p = jnp.exp(mix - top)
            total = jnp.sum(p, axis=1, keepdims=True)
            out = weigh(jnp.where(own, p, 0.0), 0, lo, hi) + weigh(jnp.where(own, 0.0, p), 2, lo, hi)
            for s, d, i, j in parts:
                p = jnp.exp(s - top)
                total += jnp.sum(p, axis=1, keepdims=True)
                out += weigh(p, d, i, j)
            out_ref[0, 0, lo:hi, :] = (out / total).astype(bf16)


def attend(at, gs, hs):
    rows = gs[0].shape[2]
    hbm = pl.BlockSpec(memory_space=pl.ANY)
    return pl.pallas_call(
        functools.partial(attend_kernel, rows // 2),
        out_shape=jax.ShapeDtypeStruct((4, 3, rows, AHD), bf16),
        grid_spec=pltpu.PrefetchScalarGridSpec(
            num_scalar_prefetch=1,
            grid=(3, 4),
            in_specs=[hbm] * 8,
            out_specs=pl.BlockSpec((1, 1, rows, AHD), lambda s, b, at: (lax.rem(at[2] - b + 4, 4), s, 0, 0)),
            scratch_shapes=[
                pltpu.VMEM((4, 3, rows, AHD), bf16),
                pltpu.VMEM((6, 2, 3, rows, AHD), bf16),
                pltpu.SemaphoreType.DMA((3, 4)),
            ],
        ),
        compiler_params=pltpu.CompilerParams(vmem_limit_bytes=40 << 20),
        cost_estimate=pl.CostEstimate(
            flops=12 * rows * rows * 10 * AHD, bytes_accessed=12 << 20, transcendentals=2 * rows * rows * 10
        ),
        name="attend",
    )(at, *gs, *hs)


def attn_cols(attn_ref, y, head, j, rows):
    low, high = lax.rem(2 * head - y + 4, 4), lax.rem(2 * head + 1 - y + 4, 4)
    half = rows // 2
    if j == 2:
        return jnp.concatenate([attn_ref[low, 2, :half], attn_ref[high, 0, half:]], axis=0).astype(f32)
    return (attn_ref[low, j] if j < 2 else attn_ref[high, j - 2]).astype(f32)


def mean_of(x, axis):
    return jnp.sum(x, axis=axis, keepdims=True) / f32(x.shape[0] if axis == 0 else x.size)


def answer(q, u, gain):
    gate = dot(q, u[0], 1, 0)
    up = dot(q, u[1], 1, 0)
    act = (gate * jax.nn.sigmoid(gate) * up).astype(bf16)
    fast = dot(act, u[2], 1, 0)
    mean = jnp.sum(fast * fast, axis=1, keepdims=True) / f32(fast.shape[1])
    return fast * lax.rsqrt(mean + EPS) * gain


def update_kernel(at_ref, rate_ref, g0, g1, g2, g3, w_ref, q_ref, gain_ref, u_ref, out_ref, d_ref):
    head, z, y = at_ref[0], at_ref[1], at_ref[2]
    part = g0.shape[2]
    for i in range(4):
        for j in range(4):
            row = pl.multiple_of((4 * lax.rem(z + i, 4) + lax.rem(y + j, 4)) * part, 8)
            for m in range(3):
                d_ref[m, pl.ds(row, part), :] = (g0, g1, g2, g3)[i][j, m].astype(f32)
    for m in range(3):
        d = d_ref[m]
        w = w_ref[0, m].astype(f32)
        ww = w * w
        col_w = mean_of(ww, 0)
        mean_w = jnp.sum(col_w, axis=1, keepdims=True) / f32(w.shape[1])
        mean_d = jnp.sum(mean_of(d * d, 0), axis=1, keepdims=True) / f32(w.shape[1])
        factor = rate_ref[head] * jnp.sqrt((mean_w + EPS) / (mean_d + EPS))
        moved = w + factor * d
        col_m = mean_of(moved * moved, 0)
        u_ref[m] = (moved * jnp.sqrt((col_w + EPS) / (col_m + EPS))).astype(bf16)
    out_ref[...] = answer(q_ref[...], u_ref, gain_ref[...]).astype(bf16)


def update_of(at, rate, sums, weights, q, gain):
    rows, width = q.shape
    whole = lambda shape: pl.BlockSpec(shape, lambda i, at, r: (0,) * len(shape))
    shapes = [jax.ShapeDtypeStruct((3, width, width), bf16), jax.ShapeDtypeStruct((rows, width), bf16)]
    return pl.pallas_call(
        update_kernel,
        out_shape=shapes,
        grid_spec=pltpu.PrefetchScalarGridSpec(
            num_scalar_prefetch=2,
            grid=(1,),
            in_specs=[
                *[whole(sums[0].shape)] * 4,
                pl.BlockSpec((1, 3, width, width), lambda i, at, r: (at[0], 0, 0, 0)),
                whole(q.shape),
                pl.BlockSpec((1, width), lambda i, at, r: (0, at[0])),
            ],
            out_specs=[whole(s.shape) for s in shapes],
            scratch_shapes=[pltpu.VMEM((3, width, width), f32)],
        ),
        compiler_params=pltpu.CompilerParams(vmem_limit_bytes=56 << 20),
        cost_estimate=pl.CostEstimate(
            flops=6 * rows * width * width, bytes_accessed=8 << 20, transcendentals=rows * width
        ),
        name="update",
    )(at, rate, *sums, weights, q, gain)


def own_kernel(at_ref, u_ref, q_ref, gain_ref, out_ref):
    out_ref[...] = answer(q_ref[...], u_ref, gain_ref[...]).astype(bf16)


def own_of(at, u, queries, gain):
    rows, width = queries.shape[0], u.shape[1]
    return pl.pallas_call(
        own_kernel,
        out_shape=jax.ShapeDtypeStruct((rows, width), bf16),
        grid_spec=pltpu.PrefetchScalarGridSpec(
            num_scalar_prefetch=1,
            grid=(1,),
            in_specs=[
                pl.BlockSpec(u.shape, lambda i, at: (0, 0, 0)),
                pl.BlockSpec((rows, width), lambda i, at: (0, at[0])),
                pl.BlockSpec((1, width), lambda i, at: (0, at[0])),
            ],
            out_specs=pl.BlockSpec((rows, width), lambda i, at: (0, 0)),
        ),
        compiler_params=pltpu.CompilerParams(vmem_limit_bytes=56 << 20),
        cost_estimate=pl.CostEstimate(
            flops=6 * rows * width * width, bytes_accessed=6 << 20, transcendentals=rows * width
        ),
        name="own",
    )(at, u, queries, gain)


def features_kernel(at_ref, f0, f1, f2, f3, near_ref, far_ref, out_ref, tmp_ref):
    y, x = at_ref[2], at_ref[3]
    rows, width = f0.shape
    for r, f in enumerate((f0, f1, f2, f3)):
        tmp_ref[lax.rem(x + r, 4)] = f[...]
    for g in range(2):

        def fill(attn_ref):
            for h in range(2):
                for j in range(width // AHD):
                    cols = slice(j * AHD, (j + 1) * AHD)
                    add = attn_cols(attn_ref, y, h, j, rows)
                    c0 = (2 * g + h) * width + j * AHD
                    out_ref[:, c0 : c0 + AHD] = (tmp_ref[2 * g + h, :, cols].astype(f32) + add).astype(bf16)

        @pl.when(x // 2 == g)
        def _():
            fill(near_ref)

        @pl.when(x // 2 != g)
        def _():
            fill(far_ref)


def features_of(at, fasts, near, far):
    rows, width = fasts[0].shape
    vmem = pl.BlockSpec(memory_space=pltpu.VMEM)
    return pl.pallas_call(
        features_kernel,
        out_shape=jax.ShapeDtypeStruct((rows, 4 * width), bf16),
        in_specs=[pl.BlockSpec(memory_space=pltpu.SMEM), *[vmem] * 6],
        out_specs=vmem,
        scratch_shapes=[pltpu.VMEM((4, rows, width), bf16)],
        compiler_params=pltpu.CompilerParams(vmem_limit_bytes=40 << 20),
        cost_estimate=pl.CostEstimate(flops=4 * rows * width, bytes_accessed=8 << 20, transcendentals=0),
        name="features",
    )(at, *fasts, near, far)


def project_kernel(at_ref, f_ref, a0, a1, a3, a2a, a2b, b0, b1, b3, b2a, b2b, out_ref, w_ref, sem):
    z, y, core = at_ref[0], at_ref[1], at_ref[2]
    width, cut = a0.shape[2], a0.shape[3]
    full = cut + b0.shape[3]

    def copy(src, half, g, zb, yb):
        c0 = g * full + half * cut
        dst = w_ref.at[lax.rem(zb, 2), pl.ds(pl.multiple_of(yb * width, 16), width), c0 : c0 + src.shape[1]]
        return pltpu.make_async_copy(src, dst, sem.at[half, g, lax.rem(zb, 2), yb])

    for i in range(4):
        for j in range(4):
            for half, (big, small) in enumerate(((z, y), (y, z))):
                far = (a2a, b2a) if j < 2 else (a2b, b2b)
                srcs = ((a0, a1, far[0], a3), (b0, b1, far[1], b3))[half]
                p, q = lax.rem(big + i, 4), lax.rem(small + j, 4)
                zb, yb = (p, q) if half == 0 else (q, p)

                @pl.when(zb // 2 == core)
                def _():
                    for g in range(2):
                        copy(srcs[i].at[j - 2 if i == 2 and j >= 2 else j, g], half, g, zb, yb).start()

    f = f_ref[...]
    for zb in range(2):
        for half, src in enumerate((a0, b0)):
            for g in range(2):
                for yb in range(4):
                    copy(src.at[0, 0], half, g, zb, yb).wait()
        cols = 4 * width
        out_ref[:, zb * cols : (zb + 1) * cols] = dot(f, w_ref[zb], 1, 1).astype(bf16)


def project(at, f, pieces):
    rows, full = f.shape
    width = pieces[0].shape[2]
    vmem = pl.BlockSpec(memory_space=pltpu.VMEM)
    hbm = pl.BlockSpec(memory_space=pl.ANY)
    return pl.pallas_call(
        project_kernel,
        out_shape=jax.ShapeDtypeStruct((rows, 8 * width), bf16),
        in_specs=[pl.BlockSpec(memory_space=pltpu.SMEM), vmem, *[hbm] * 10],
        out_specs=vmem,
        scratch_shapes=[pltpu.VMEM((2, 4 * width, full), bf16), pltpu.SemaphoreType.DMA((2, 2, 2, 4))],
        compiler_params=pltpu.CompilerParams(vmem_limit_bytes=40 << 20),
        cost_estimate=pl.CostEstimate(
            flops=2 * rows * full * 8 * width, bytes_accessed=10 << 20, transcendentals=0
        ),
        name="project",
    )(at, f, *pieces)


def scatter(chunks, axis):
    total = chunks[0].astype(f32)
    got = [hop(chunks[k], axis, k) for k in (1, 3, 2)]
    for g in got:
        total = total + g.astype(f32)
    return total.astype(bf16)


def gather(block, axis):
    got = {k: hop(block, axis, -k) for k in (1, 3, 2)}
    return [block, got[1], got[2], got[3]]


def gather_ring(block, axis):
    up, down = hop(block, axis, -1), hop(block, axis, 1)
    return (block, up, down, hop(up[:2], axis, -1), hop(down[2:], axis, 1))


def body(queries, keys, values, token_rate, head_rate, fast_weights, ttt_gain, out_weight):
    xl, z, y = lax.axis_index("xl"), lax.axis_index("z"), lax.axis_index("y")
    xh, core = lax.axis_index("xh"), lax.axis_index("core")
    x = 2 * xh + xl
    width = fast_weights.shape[2]
    at = jnp.stack([xl, z, y, x]).astype(jnp.int32)

    def cols_of(a, head):
        return lax.dynamic_slice_in_dim(a, head * width, width, 1)

    def target_of(head):
        rate = lax.dynamic_slice_in_dim(token_rate, head, 1, 1)
        return (rate * cols_of(values, head).astype(f32)).astype(bf16)

    k_got = hop(cols_of(keys, 1 - xl), "xl", 1)
    t_got = hop(target_of(1 - xl), "xl", 1)

    turned = out_weight.T
    one = along_x(turned, [(2, 0), (0, 1), (1, 2)])
    two = along_x(turned, [(2, 1), (3, 2), (1, 3)])

    packs = pack(at, queries, keys, values)
    gs = [packs[0]] + [hop(packs[k], "y", k) for k in range(1, 4)]
    sofar = descent_of(at, keys, target_of(xl), fast_weights)
    parts = descent_of(at, k_got, t_got, fast_weights, sofar)

    low = jnp.where(x == 0, turned, jnp.where(x == 3, two, one))
    high = jnp.where(x == 3, turned, jnp.where(x == 0, one, two))
    pair = jnp.stack([low, high])
    block_a = jnp.stack(gather(pair[:, :, :width], "y"))
    block_b = jnp.stack(gather(pair[:, :, width:], "z"))
    queries_far = lax.optimization_barrier((queries, t_got))[0]
    q_got = hop(cols_of(queries_far, 1 - xl), "xl", 1)

    parts = scatter(parts, "z")
    pieces = (*gather_ring(block_a, "z"), *gather_ring(block_b, "y"))

    hs = [next_ring(gs[k][1:], k) for k in range(4)]

    sums = scatter(parts, "y")
    sums = gather(jnp.stack(gather(sums, "y")), "z")

    done = attend(at, gs, hs)
    near = jnp.stack([done[0]] + [hop(done[k], "y", -k) for k in range(1, 4)])
    far = hop(near, "xh", 1)
    gain = ttt_gain[None, :]
    new, fast = update_of(at, head_rate, sums, fast_weights, q_got, gain)
    next_fast = along_x(fast, [(i, (i + 3) % 4) for i in range(4)])
    last_fast = along_x(fast, [(i, (i + 1) % 4) for i in range(4)])
    mine_fast = own_of(at, new, queries, gain)
    far_fast = hop(mine_fast, "xh", 1)
    f = features_of(at, (mine_fast, next_fast, far_fast, last_fast), near, far)

    def at_of(place):
        return jnp.stack([z, y, place]).astype(jnp.int32)

    sent = project(at_of(1 - core), f, pieces)
    got = hop(sent, "core", 1)
    f = lax.optimization_barrier((f, sent))[0]
    mine = project(at_of(core), f, pieces)
    return (mine.astype(f32) + got.astype(f32)).astype(bf16)


def solution(mesh):
    fine = Mesh(mesh.devices.reshape(2, 4, 4, 2, 2), ("xl", "z", "y", "xh", "core"))
    seq, head = ("xl", "z", "y"), ("xh", "core")
    placed = (
        P(seq, head),
        P(seq, head),
        P(seq, head),
        P(seq, head),
        P(head),
        P(head, None, None, None),
        P(head),
        P(head, seq),
    )
    return jax.shard_map(body, mesh=fine, in_specs=placed, out_specs=P(seq, head), check_vma=False)
```

```python
import functools

import jax
import jax.numpy as jnp
from jax import lax
from jax.experimental import pallas as pl
from jax.experimental.pallas import tpu as pltpu
from jax.sharding import Mesh, PartitionSpec as P


AHD = 128
EPS = 1e-06
f32 = jnp.float32
bf16 = jnp.bfloat16


def hop(block, axis, distance):
    n = lax.axis_size(axis)
    return lax.ppermute(block, axis, [(i, (i + distance) % n) for i in range(n)])


def along_x(block, route):
    place = (0, 2, 1, 3)
    return lax.ppermute(block, ("xl", "xh"), [(place[a], place[b]) for a, b in route])


def next_ring(block, distance):
    axes = ("xl", "z", "y")
    route = [(i, i + 4) for i in range(28) if (i - distance) % 4 >= 2]
    return lax.ppermute(block, axes, route)


def dot(a, b, ca, cb):
    return lax.dot_general(a, b, (((ca,), (cb,)), ((), ())), preferred_element_type=f32)


def descent_kernel(at_ref, k_ref, t_ref, kg_ref, tg_ref, w_ref, out_ref, d_ref):
    first = pl.program_id(0) == 0
    k = jnp.where(first, k_ref[...], kg_ref[...])
    target = jnp.where(first, t_ref[...], tg_ref[...])
    gate = dot(k, w_ref[0, 0], 1, 0)
    up = dot(k, w_ref[0, 1], 1, 0)
    back = dot(target, w_ref[0, 2], 1, 1)
    s = jax.nn.sigmoid(gate)
    silu = gate * s
    act = (silu * up).astype(bf16)
    grad_gate = (back * up * (s * (1.0 + gate * (1.0 - s)))).astype(bf16)
    grad_up = (back * silu).astype(bf16)
    pairs = ((k, grad_gate), (k, grad_up), (act, target))
    for m, (a, b) in enumerate(pairs):
        d_ref[m] = dot(a, b, 0, 0) + jnp.where(first, 0.0, d_ref[m])

    @pl.when(jnp.logical_not(first))
    def _():
        z, y = at_ref[1], at_ref[2]
        part = out_ref.shape[3]
        for i in range(4):
            for j in range(4):
                row = (4 * i + j) * part
                for m in range(3):
                    block = d_ref[m, row : row + part, :].astype(bf16)
                    out_ref[lax.rem(i - z + 4, 4), lax.rem(j - y + 4, 4), m] = block


def descent_of(at, keys, target, k_got, t_got, weights):
    rows, width = target.shape
    whole = lambda shape: pl.BlockSpec(shape, lambda i, at: (0,) * len(shape))
    out = jax.ShapeDtypeStruct((4, 4, 3, width // 16, width), bf16)
    return pl.pallas_call(
        descent_kernel,
        out_shape=out,
        grid_spec=pltpu.PrefetchScalarGridSpec(
            num_scalar_prefetch=1,
            grid=(2,),
            in_specs=[
                pl.BlockSpec((rows, width), lambda i, at: (0, at[0])),
                *[whole((rows, width))] * 3,
                pl.BlockSpec((1, 3, width, width), lambda i, at: (at[0], 0, 0, 0)),
            ],
            out_specs=whole(out.shape),
            scratch_shapes=[pltpu.VMEM((3, width, width), f32)],
        ),
        compiler_params=pltpu.CompilerParams(vmem_limit_bytes=56 << 20),
        cost_estimate=pl.CostEstimate(
            flops=24 * rows * width * width, bytes_accessed=8 << 20, transcendentals=2 * rows * width
        ),
        name="descent",
    )(at, keys, target, k_got, t_got, weights)


def start_of(d):
    return 2 * d + jnp.where(d >= 2, 1, 0)


def pack_kernel(at_ref, *refs):
    ins, outs = refs[:12], refs[12:]
    for k in range(4):
        for i in range(3):
            outs[k][i, 0] = ins[3 * k + i][...]


def pack(at, queries, keys, values):
    rows = queries.shape[0]

    def spec(k):
        return pl.BlockSpec((rows, AHD), lambda s, at: (0, start_of(lax.rem(at[2] + k, 4)) + s))

    out = pl.BlockSpec((3, 1, rows, AHD), lambda s, at: (0, s, 0, 0))
    return pl.pallas_call(
        pack_kernel,
        out_shape=[jax.ShapeDtypeStruct((3, 3, rows, AHD), bf16)] * 4,
        grid_spec=pltpu.PrefetchScalarGridSpec(
            num_scalar_prefetch=1,
            grid=(3,),
            in_specs=[spec(k) for k in range(4) for _ in range(3)],
            out_specs=[out] * 4,
        ),
        cost_estimate=pl.CostEstimate(flops=0, bytes_accessed=10 << 20, transcendentals=0),
        name="pack",
    )(at, *[queries, keys, values] * 4)


def attend_kernel(tile, at_ref, g0, g1, g2, g3, h0, h1, h2, h3, out_ref, q_ref, kv_ref, sems):
    xl, z, y = at_ref[0], at_ref[1], at_ref[2]
    slot, yb = pl.program_id(0), pl.program_id(1)

    def copies(act):
        for k in range(4):
            at = lax.rem(y - k + 4, 4)
            g, h = (g0, g1, g2, g3)[k], (h0, h1, h2, h3)[k]
            act(pltpu.make_async_copy(g.at[0], q_ref.at[at], sems.at[0, k]))
            act(pltpu.make_async_copy(g.at[pl.ds(1, 2)], kv_ref.at[at + 2], sems.at[1, k]))

            @pl.when(at >= 2)
            def _():
                act(pltpu.make_async_copy(h, kv_ref.at[at - 2], sems.at[2, k]))

    @pl.when((slot == 0) & (yb == 0))
    def _():
        copies(lambda c: c.start())
        copies(lambda c: c.wait())

    neg = f32(-1e30)
    first = (xl == 0) & (z == 0)
    bias1 = jnp.where(first & (yb < 1), neg, f32(0))
    bias2 = jnp.where(first & (yb < 2), neg, f32(0))
    scale = f32(1.0) / jnp.sqrt(f32(AHD))
    row = lax.broadcasted_iota(jnp.int32, (tile, tile), 0)
    col = lax.broadcasted_iota(jnp.int32, (tile, tile), 1)
    own = col <= row
    odd = lax.rem(y, 2)
    shared = slot == 2 - 2 * odd

    def step(t, _):
        here, other = pl.ds(pl.multiple_of(t * tile, tile), tile), pl.ds(pl.multiple_of((1 - t) * tile, tile), tile)
        q = q_ref[yb, slot, here, :]

        def score(d, cols):
            return dot(q, kv_ref[yb + 2 - d, 0, slot, cols, :], 1, 1) * scale

        def weigh(p, d, cols):
            return dot(p.astype(bf16), kv_ref[yb + 2 - d, 1, slot, cols, :], 1, 0)

        edge = 2 - 2 * t
        s0 = jnp.where(own, score(0, here), score(2, here) + bias2)
        s1 = score(1, slice(None)) + bias1
        s2 = score(edge, other) + jnp.where(t == 0, bias2, f32(0))
        top = jnp.maximum(jnp.max(s0, axis=1, keepdims=True), jnp.max(s1, axis=1, keepdims=True))
        top = jnp.maximum(top, jnp.max(s2, axis=1, keepdims=True))
        p0, p1, p2 = jnp.exp(s0 - top), jnp.exp(s1 - top), jnp.exp(s2 - top)
        total = sum(jnp.sum(p, axis=1, keepdims=True) for p in (p0, p1, p2))
        out = weigh(jnp.where(own, p0, 0.0), 0, here) + weigh(jnp.where(own, 0.0, p0), 2, here)
        out += weigh(p1, 1, slice(None)) + weigh(p2, edge, other)
        out_ref[0, 0, here, :] = (out / total).astype(bf16)
        return 0

    lax.fori_loop(jnp.where(shared, odd, 0), jnp.where(shared, odd + 1, 2), step, 0)


def attend(at, gs, hs):
    rows = gs[0].shape[2]
    hbm = pl.BlockSpec(memory_space=pl.ANY)
    return pl.pallas_call(
        functools.partial(attend_kernel, rows // 2),
        out_shape=jax.ShapeDtypeStruct((4, 3, rows, AHD), bf16),
        grid_spec=pltpu.PrefetchScalarGridSpec(
            num_scalar_prefetch=1,
            grid=(3, 4),
            in_specs=[hbm] * 8,
            out_specs=pl.BlockSpec((1, 1, rows, AHD), lambda s, b, at: (lax.rem(at[2] - b + 4, 4), s, 0, 0)),
            scratch_shapes=[
                pltpu.VMEM((4, 3, rows, AHD), bf16),
                pltpu.VMEM((6, 2, 3, rows, AHD), bf16),
                pltpu.SemaphoreType.DMA((3, 4)),
            ],
        ),
        compiler_params=pltpu.CompilerParams(vmem_limit_bytes=40 << 20),
        cost_estimate=pl.CostEstimate(
            flops=12 * rows * rows * 10 * AHD, bytes_accessed=12 << 20, transcendentals=2 * rows * rows * 10
        ),
        name="attend",
    )(at, *gs, *hs)


def columns_kernel(at_ref, r0, r1, r2, r3, own_ref, other_ref, all_ref):
    xl, y = at_ref[0], at_ref[2]
    for k, r in enumerate((r0, r1, r2, r3)):
        all_ref[k] = r[...]
    half = r0.shape[1] // 2
    for head, out_ref in ((xl, own_ref), (1 - xl, other_ref)):
        low, high = lax.rem(2 * head - y + 4, 4), lax.rem(2 * head + 1 - y + 4, 4)
        for j in range(2):
            out_ref[:, j * AHD : (j + 1) * AHD] = all_ref[low, j]
            out_ref[:, (j + 3) * AHD : (j + 4) * AHD] = all_ref[high, j + 1]
        out_ref[:half, 2 * AHD : 3 * AHD] = all_ref[low, 2, :half]
        out_ref[half:, 2 * AHD : 3 * AHD] = all_ref[high, 0, half:]


def columns_of(at, backs):
    rows = backs[0].shape[1]
    vmem = pl.BlockSpec(memory_space=pltpu.VMEM)
    return pl.pallas_call(
        columns_kernel,
        out_shape=[jax.ShapeDtypeStruct((rows, 5 * AHD), bf16)] * 2,
        in_specs=[pl.BlockSpec(memory_space=pltpu.SMEM), *[vmem] * 4],
        out_specs=[vmem] * 2,
        scratch_shapes=[pltpu.VMEM((4, *backs[0].shape), bf16)],
        cost_estimate=pl.CostEstimate(flops=0, bytes_accessed=3 << 20, transcendentals=0),
        name="columns",
    )(at, *backs)


def mean_of(x, axis):
    return jnp.sum(x, axis=axis, keepdims=True) / f32(x.shape[0] if axis == 0 else x.size)


def answer(q, u, gain):
    gate = dot(q, u[0], 1, 0)
    up = dot(q, u[1], 1, 0)
    act = (gate * jax.nn.sigmoid(gate) * up).astype(bf16)
    fast = dot(act, u[2], 1, 0)
    mean = jnp.sum(fast * fast, axis=1, keepdims=True) / f32(fast.shape[1])
    return fast * lax.rsqrt(mean + EPS) * gain


def update_kernel(at_ref, rate_ref, g0, g1, g2, g3, w_ref, q_ref, gain_ref, u_ref, out_ref, d_ref):
    head, z, y = at_ref[0], at_ref[1], at_ref[2]
    part = g0.shape[2]
    for i in range(4):
        for j in range(4):
            row = pl.multiple_of((4 * lax.rem(z + i, 4) + lax.rem(y + j, 4)) * part, 8)
            for m in range(3):
                d_ref[m, pl.ds(row, part), :] = (g0, g1, g2, g3)[i][j, m].astype(f32)
    for m in range(3):
        d = d_ref[m]
        w = w_ref[0, m].astype(f32)
        ww = w * w
        col_w = mean_of(ww, 0)
        mean_w = jnp.sum(col_w, axis=1, keepdims=True) / f32(w.shape[1])
        mean_d = jnp.sum(mean_of(d * d, 0), axis=1, keepdims=True) / f32(w.shape[1])
        factor = rate_ref[head] * jnp.sqrt((mean_w + EPS) / (mean_d + EPS))
        moved = w + factor * d
        col_m = mean_of(moved * moved, 0)
        u_ref[m] = (moved * jnp.sqrt((col_w + EPS) / (col_m + EPS))).astype(bf16)
    out_ref[...] = answer(q_ref[...], u_ref, gain_ref[...])


def update_of(at, rate, sums, weights, q, gain):
    rows, width = q.shape
    whole = lambda shape: pl.BlockSpec(shape, lambda i, at, r: (0,) * len(shape))
    shapes = [jax.ShapeDtypeStruct((3, width, width), bf16), jax.ShapeDtypeStruct((rows, width), f32)]
    return pl.pallas_call(
        update_kernel,
        out_shape=shapes,
        grid_spec=pltpu.PrefetchScalarGridSpec(
            num_scalar_prefetch=2,
            grid=(1,),
            in_specs=[
                *[whole(sums[0].shape)] * 4,
                pl.BlockSpec((1, 3, width, width), lambda i, at, r: (at[0], 0, 0, 0)),
                whole(q.shape),
                pl.BlockSpec((1, width), lambda i, at, r: (0, at[0])),
            ],
            out_specs=[whole(s.shape) for s in shapes],
            scratch_shapes=[pltpu.VMEM((3, width, width), f32)],
        ),
        compiler_params=pltpu.CompilerParams(vmem_limit_bytes=56 << 20),
        cost_estimate=pl.CostEstimate(
            flops=6 * rows * width * width, bytes_accessed=8 << 20, transcendentals=rows * width
        ),
        name="update",
    )(at, rate, *sums, weights, q, gain)


def own_kernel(at_ref, u_ref, q_ref, gain_ref, attn_ref, out_ref):
    out_ref[...] = (answer(q_ref[...], u_ref, gain_ref[...]) + attn_ref[...].astype(f32)).astype(bf16)


def own_of(at, u, queries, gain, attn):
    rows, width = attn.shape
    return pl.pallas_call(
        own_kernel,
        out_shape=jax.ShapeDtypeStruct((rows, width), bf16),
        grid_spec=pltpu.PrefetchScalarGridSpec(
            num_scalar_prefetch=1,
            grid=(1,),
            in_specs=[
                pl.BlockSpec(u.shape, lambda i, at: (0, 0, 0)),
                pl.BlockSpec((rows, width), lambda i, at: (0, at[0])),
                pl.BlockSpec((1, width), lambda i, at: (0, at[0])),
                pl.BlockSpec((rows, width), lambda i, at: (0, 0)),
            ],
            out_specs=pl.BlockSpec((rows, width), lambda i, at: (0, 0)),
        ),
        compiler_params=pltpu.CompilerParams(vmem_limit_bytes=56 << 20),
        cost_estimate=pl.CostEstimate(
            flops=6 * rows * width * width, bytes_accessed=6 << 20, transcendentals=rows * width
        ),
        name="own",
    )(at, u, queries, gain, attn)


def project_kernel(at_ref, f0, f1, f2, f3, a0, a1, a3, a2a, a2b, b0, b1, b3, b2a, b2b, out_ref, w_ref, f_ref, sem):
    z, y, core, x = at_ref[0], at_ref[1], at_ref[2], at_ref[3]
    width, cut = a0.shape[2], a0.shape[3]
    full = cut + b0.shape[3]

    def copy(src, half, g, zb, yb):
        c0 = g * full + half * cut
        row = pl.multiple_of((4 * lax.rem(zb, 2) + yb) * width, 16)
        dst = w_ref.at[pl.ds(row, width), c0 : c0 + src.shape[1]]
        return pltpu.make_async_copy(src, dst, sem.at[half, g, lax.rem(zb, 2), yb])

    for i in range(4):
        for j in range(4):
            for half, (big, small) in enumerate(((z, y), (y, z))):
                far = (a2a, b2a) if j < 2 else (a2b, b2b)
                srcs = ((a0, a1, far[0], a3), (b0, b1, far[1], b3))[half]
                p, q = lax.rem(big + i, 4), lax.rem(small + j, 4)
                zb, yb = (p, q) if half == 0 else (q, p)

                @pl.when(zb // 2 == core)
                def _():
                    for g in range(2):
                        copy(srcs[i].at[j - 2 if i == 2 and j >= 2 else j, g], half, g, zb, yb).start()

    for r, f in enumerate((f0, f1, f2, f3)):
        cols = pl.multiple_of(lax.rem(x + r, 4) * f.shape[1], AHD)
        f_ref[:, pl.ds(cols, f.shape[1])] = f[...]

    def arrive(zb):
        for half, src in enumerate((a0, b0)):
            for g in range(2):
                for yb in range(4):
                    copy(src.at[0, 0], half, g, zb, yb).wait()

    def tile(t, _):
        @pl.when(t == 0)
        def _():
            arrive(0)

        @pl.when(t == 2)
        def _():
            arrive(1)

        cols = pl.ds(pl.multiple_of(t * 2 * AHD, 2 * AHD), 2 * AHD)
        out_ref[:, cols] = dot(f_ref[...], w_ref[cols, :], 1, 1).astype(bf16)
        return 0

    lax.fori_loop(0, out_ref.shape[1] // (2 * AHD), tile, 0)


def project(at, fs, pieces):
    rows, full = fs[0].shape[0], 4 * fs[0].shape[1]
    width = pieces[0].shape[2]
    vmem = pl.BlockSpec(memory_space=pltpu.VMEM)
    hbm = pl.BlockSpec(memory_space=pl.ANY)
    return pl.pallas_call(
        project_kernel,
        out_shape=jax.ShapeDtypeStruct((rows, 8 * width), bf16),
        in_specs=[pl.BlockSpec(memory_space=pltpu.SMEM), *[vmem] * 4, *[hbm] * 10],
        out_specs=vmem,
        scratch_shapes=[
            pltpu.VMEM((8 * width, full), bf16),
            pltpu.VMEM((rows, full), bf16),
            pltpu.SemaphoreType.DMA((2, 2, 2, 4)),
        ],
        compiler_params=pltpu.CompilerParams(vmem_limit_bytes=40 << 20),
        cost_estimate=pl.CostEstimate(
            flops=2 * rows * full * 8 * width, bytes_accessed=10 << 20, transcendentals=0
        ),
        name="project",
    )(at, *fs, *pieces)


def scatter(chunks, axis):
    total = chunks[0].astype(f32)
    got = [hop(chunks[k], axis, k) for k in (1, 3, 2)]
    for g in got:
        total = total + g.astype(f32)
    return total.astype(bf16)


def gather(block, axis):
    got = {k: hop(block, axis, -k) for k in (1, 3, 2)}
    return [block, got[1], got[2], got[3]]


def gather_ring(block, axis):
    up, down = hop(block, axis, -1), hop(block, axis, 1)
    return (block, up, down, hop(up[:2], axis, -1), hop(down[2:], axis, 1))


def body(queries, keys, values, token_rate, head_rate, fast_weights, ttt_gain, out_weight):
    xl, z, y = lax.axis_index("xl"), lax.axis_index("z"), lax.axis_index("y")
    xh, core = lax.axis_index("xh"), lax.axis_index("core")
    x = 2 * xh + xl
    width = fast_weights.shape[2]
    at = jnp.stack([xl, z, y, x]).astype(jnp.int32)

    def cols_of(a, head):
        return lax.dynamic_slice_in_dim(a, head * width, width, 1)

    def target_of(head):
        rate = lax.dynamic_slice_in_dim(token_rate, head, 1, 1)
        return (rate * cols_of(values, head).astype(f32)).astype(bf16)

    k_got = hop(cols_of(keys, 1 - xl), "xl", 1)
    t_got = hop(target_of(1 - xl), "xl", 1)

    turned = out_weight.T
    one = along_x(turned, [(2, 0), (0, 1), (1, 2)])
    two = along_x(turned, [(2, 1), (3, 2), (1, 3)])

    packs = pack(at, queries, keys, values)
    gs = [packs[0]] + [hop(packs[k], "y", k) for k in range(1, 4)]
    parts = descent_of(at, keys, target_of(xl), k_got, t_got, fast_weights)

    low = jnp.where(x == 0, turned, jnp.where(x == 3, two, one))
    high = jnp.where(x == 3, turned, jnp.where(x == 0, one, two))
    pair = jnp.stack([low, high])
    block_a = jnp.stack(gather(pair[:, :, :width], "y"))
    block_b = jnp.stack(gather(pair[:, :, width:], "z"))
    queries_far = lax.optimization_barrier((queries, t_got))[0]
    q_got = hop(cols_of(queries_far, 1 - xl), "xl", 1)

    parts = scatter(parts, "z")
    pieces = (*gather_ring(block_a, "z"), *gather_ring(block_b, "y"))

    hs = [next_ring(gs[k][1:], k) for k in range(4)]

    sums = scatter(parts, "y")
    sums = gather(jnp.stack(gather(sums, "y")), "z")

    done = attend(at, gs, hs)
    backs = [done[0]] + [hop(done[k], "y", -k) for k in range(1, 4)]
    attn, other = columns_of(at, backs)
    attn_got = hop(other, "xl", 1)
    gain = ttt_gain[None, :]
    new, fast = update_of(at, head_rate, sums, fast_weights, q_got, gain)
    fast = (fast + attn_got.astype(f32)).astype(bf16)
    next_fast = along_x(fast, [(i, (i + 3) % 4) for i in range(4)])
    last_fast = along_x(fast, [(i, (i + 1) % 4) for i in range(4)])
    mine_fast = own_of(at, new, queries, gain, attn)
    far_fast = hop(mine_fast, "xh", 1)
    fs = (mine_fast, next_fast, far_fast, last_fast)

    def at_of(place):
        return jnp.stack([z, y, place, x]).astype(jnp.int32)

    sent = project(at_of(1 - core), fs, pieces)
    got = hop(sent, "core", 1)
    fs = lax.optimization_barrier((*fs, sent))[:4]
    mine = project(at_of(core), fs, pieces)
    return (mine.astype(f32) + got.astype(f32)).astype(bf16)


def solution(mesh):
    fine = Mesh(mesh.devices.reshape(2, 4, 4, 2, 2), ("xl", "z", "y", "xh", "core"))
    seq, head = ("xl", "z", "y"), ("xh", "core")
    placed = (
        P(seq, head),
        P(seq, head),
        P(seq, head),
        P(seq, head),
        P(head),
        P(head, None, None, None),
        P(head),
        P(head, seq),
    )
    return jax.shard_map(body, mesh=fine, in_specs=placed, out_specs=P(seq, head), check_vma=False)
```

```python
import functools
import math

import jax
import jax.numpy as jnp
from jax import lax
from jax.experimental import pallas as pl
from jax.experimental.pallas import tpu as pltpu
from jax.sharding import Mesh, PartitionSpec as P


AHD = 128
EPS = 1e-06
CUT = 6
f32 = jnp.float32
bf16 = jnp.bfloat16


def hop(block, axis, distance):
    n = lax.axis_size(axis)
    return lax.ppermute(block, axis, [(i, (i + distance) % n) for i in range(n)])


def along_x(block, route):
    place = (0, 2, 1, 3)
    return lax.ppermute(block, ("xl", "xh"), [(place[a], place[b]) for a, b in route])


def next_ring(block, distance):
    axes = ("xl", "z", "y")
    route = [(i, i + 4) for i in range(28) if (i - distance) % 4 >= 2]
    return lax.ppermute(block, axes, route)


def dot(a, b, ca, cb):
    return lax.dot_general(a, b, (((ca,), (cb,)), ((), ())), preferred_element_type=f32)


def descent_kernel(at_ref, k_ref, t_ref, kg_ref, tg_ref, w_ref, out_ref, d_ref):
    first = pl.program_id(0) == 0
    k = jnp.where(first, k_ref[...], kg_ref[...])
    target = jnp.where(first, t_ref[...], tg_ref[...])
    gate = dot(k, w_ref[0, 0], 1, 0)
    up = dot(k, w_ref[0, 1], 1, 0)
    back = dot(target, w_ref[0, 2], 1, 1)
    s = jax.nn.sigmoid(gate)
    silu = gate * s
    act = (silu * up).astype(bf16)
    grad_gate = (back * up * (s * (1.0 + gate * (1.0 - s)))).astype(bf16)
    grad_up = (back * silu).astype(bf16)
    pairs = ((k, grad_gate), (k, grad_up), (act, target))
    for m, (a, b) in enumerate(pairs):
        d_ref[m] = dot(a, b, 0, 0) + jnp.where(first, 0.0, d_ref[m])

    @pl.when(jnp.logical_not(first))
    def _():
        z, y = at_ref[1], at_ref[2]
        part = out_ref.shape[3]
        for i in range(4):
            for j in range(4):
                row = (4 * i + j) * part
                for m in range(3):
                    block = d_ref[m, row : row + part, :].astype(bf16)
                    out_ref[lax.rem(i - z + 4, 4), lax.rem(j - y + 4, 4), m] = block


def descent_of(at, keys, target, k_got, t_got, weights):
    rows, width = target.shape
    whole = lambda shape: pl.BlockSpec(shape, lambda i, at: (0,) * len(shape))
    out = jax.ShapeDtypeStruct((4, 4, 3, width // 16, width), bf16)
    return pl.pallas_call(
        descent_kernel,
        out_shape=out,
        grid_spec=pltpu.PrefetchScalarGridSpec(
            num_scalar_prefetch=1,
            grid=(2,),
            in_specs=[
                pl.BlockSpec((rows, width), lambda i, at: (0, at[0])),
                *[whole((rows, width))] * 3,
                pl.BlockSpec((1, 3, width, width), lambda i, at: (at[0], 0, 0, 0)),
            ],
            out_specs=whole(out.shape),
            scratch_shapes=[pltpu.VMEM((3, width, width), f32)],
        ),
        compiler_params=pltpu.CompilerParams(vmem_limit_bytes=56 << 20),
        cost_estimate=pl.CostEstimate(
            flops=24 * rows * width * width, bytes_accessed=8 << 20, transcendentals=2 * rows * width
        ),
        name="descent",
    )(at, keys, target, k_got, t_got, weights)


def start_of(d):
    return 2 * d + jnp.where(d >= 2, 1, 0)


def pack_kernel(at_ref, *refs):
    ins, outs = refs[:12], refs[12:]
    for k in range(4):
        for i in range(3):
            outs[k][i, 0] = ins[3 * k + i][...]


def pack(at, queries, keys, values):
    rows = queries.shape[0]

    def spec(k):
        return pl.BlockSpec((rows, AHD), lambda s, at: (0, start_of(lax.rem(at[2] + k, 4)) + s))

    out = pl.BlockSpec((3, 1, rows, AHD), lambda s, at: (0, s, 0, 0))
    return pl.pallas_call(
        pack_kernel,
        out_shape=[jax.ShapeDtypeStruct((3, 3, rows, AHD), bf16)] * 4,
        grid_spec=pltpu.PrefetchScalarGridSpec(
            num_scalar_prefetch=1,
            grid=(3,),
            in_specs=[spec(k) for k in range(4) for _ in range(3)],
            out_specs=[out] * 4,
        ),
        cost_estimate=pl.CostEstimate(flops=0, bytes_accessed=10 << 20, transcendentals=0),
        name="pack",
    )(at, *[queries, keys, values] * 4)


def attend_kernel(tile, at_ref, g0, g1, g2, g3, h0, h1, h2, h3, out_ref, q_ref, kv_ref, sems):
    xl, z, y = at_ref[0], at_ref[1], at_ref[2]
    slot, yb = pl.program_id(0), pl.program_id(1)

    def copies(act):
        for k in range(4):
            at = lax.rem(y - k + 4, 4)
            g, h = (g0, g1, g2, g3)[k], (h0, h1, h2, h3)[k]
            act(pltpu.make_async_copy(g.at[0], q_ref.at[at], sems.at[0, k]))
            act(pltpu.make_async_copy(g.at[pl.ds(1, 2)], kv_ref.at[at + 2], sems.at[1, k]))

            @pl.when(at >= 2)
            def _():
                act(pltpu.make_async_copy(h, kv_ref.at[at - 2], sems.at[2, k]))

    @pl.when((slot == 0) & (yb == 0))
    def _():
        copies(lambda c: c.start())
        copies(lambda c: c.wait())

    neg = f32(-1e30)
    first = (xl == 0) & (z == 0)
    bias1 = jnp.where(first & (yb < 1), neg, f32(0))
    bias2 = jnp.where(first & (yb < 2), neg, f32(0))
    scale = f32(math.log2(math.e) / math.sqrt(AHD))
    row = lax.broadcasted_iota(jnp.int32, (tile, tile), 0)
    col = lax.broadcasted_iota(jnp.int32, (tile, tile), 1)
    own = col <= row
    odd = lax.rem(y, 2)
    shared = slot == 2 - 2 * odd

    def step(t, _):
        here, other = pl.ds(pl.multiple_of(t * tile, tile), tile), pl.ds(pl.multiple_of((1 - t) * tile, tile), tile)
        q = q_ref[yb, slot, here, :]

        def score(d, cols):
            return dot(q, kv_ref[yb + 2 - d, 0, slot, cols, :], 1, 1)

        def weigh(p, d, cols):
            return dot(p.astype(bf16), kv_ref[yb + 2 - d, 1, slot, cols, :], 1, 0)

        edge = 2 - 2 * t
        s0 = jnp.where(own, score(0, here), score(2, here) + bias2)
        s1 = score(1, slice(None)) + bias1
        s2 = score(edge, other) + jnp.where(t == 0, bias2, f32(0))
        top = jnp.maximum(jnp.max(s0, axis=1, keepdims=True), jnp.max(s1, axis=1, keepdims=True))
        top = jnp.maximum(top, jnp.max(s2, axis=1, keepdims=True))
        p0, p1, p2 = (jnp.exp2((s - top) * scale) for s in (s0, s1, s2))
        total = sum(jnp.sum(p, axis=1, keepdims=True) for p in (p0, p1, p2))
        out = weigh(jnp.where(own, p0, 0.0), 0, here) + weigh(jnp.where(own, 0.0, p0), 2, here)
        out += weigh(p1, 1, slice(None)) + weigh(p2, edge, other)
        out_ref[0, 0, here, :] = (out / total).astype(bf16)
        return 0

    lax.fori_loop(jnp.where(shared, odd, 0), jnp.where(shared, odd + 1, 2), step, 0)


def attend(at, gs, hs):
    rows = gs[0].shape[2]
    hbm = pl.BlockSpec(memory_space=pl.ANY)
    return pl.pallas_call(
        functools.partial(attend_kernel, rows // 2),
        out_shape=jax.ShapeDtypeStruct((4, 3, rows, AHD), bf16),
        grid_spec=pltpu.PrefetchScalarGridSpec(
            num_scalar_prefetch=1,
            grid=(3, 4),
            in_specs=[hbm] * 8,
            out_specs=pl.BlockSpec((1, 1, rows, AHD), lambda s, b, at: (lax.rem(at[2] - b + 4, 4), s, 0, 0)),
            scratch_shapes=[
                pltpu.VMEM((4, 3, rows, AHD), bf16),
                pltpu.VMEM((6, 2, 3, rows, AHD), bf16),
                pltpu.SemaphoreType.DMA((3, 4)),
            ],
        ),
        compiler_params=pltpu.CompilerParams(vmem_limit_bytes=40 << 20),
        cost_estimate=pl.CostEstimate(
            flops=12 * rows * rows * 10 * AHD, bytes_accessed=12 << 20, transcendentals=2 * rows * rows * 10
        ),
        name="attend",
    )(at, *gs, *hs)


def columns_kernel(at_ref, r0, r1, r2, r3, own_ref, other_ref, all_ref):
    xl, y = at_ref[0], at_ref[2]
    for k, r in enumerate((r0, r1, r2, r3)):
        all_ref[k] = r[...]
    half = r0.shape[1] // 2
    for head, out_ref in ((xl, own_ref), (1 - xl, other_ref)):
        low, high = lax.rem(2 * head - y + 4, 4), lax.rem(2 * head + 1 - y + 4, 4)
        for j in range(2):
            out_ref[:, j * AHD : (j + 1) * AHD] = all_ref[low, j]
            out_ref[:, (j + 3) * AHD : (j + 4) * AHD] = all_ref[high, j + 1]
        out_ref[:half, 2 * AHD : 3 * AHD] = all_ref[low, 2, :half]
        out_ref[half:, 2 * AHD : 3 * AHD] = all_ref[high, 0, half:]


def columns_of(at, backs):
    rows = backs[0].shape[1]
    vmem = pl.BlockSpec(memory_space=pltpu.VMEM)
    return pl.pallas_call(
        columns_kernel,
        out_shape=[jax.ShapeDtypeStruct((rows, 5 * AHD), bf16)] * 2,
        in_specs=[pl.BlockSpec(memory_space=pltpu.SMEM), *[vmem] * 4],
        out_specs=[vmem] * 2,
        scratch_shapes=[pltpu.VMEM((4, *backs[0].shape), bf16)],
        cost_estimate=pl.CostEstimate(flops=0, bytes_accessed=3 << 20, transcendentals=0),
        name="columns",
    )(at, *backs)


def mean_of(x, axis):
    return jnp.sum(x, axis=axis, keepdims=True) / f32(x.shape[0] if axis == 0 else x.size)


def answer(q, u, gain):
    gate = dot(q, u[0], 1, 0)
    up = dot(q, u[1], 1, 0)
    act = (gate * jax.nn.sigmoid(gate) * up).astype(bf16)
    fast = dot(act, u[2], 1, 0)
    mean = jnp.sum(fast * fast, axis=1, keepdims=True) / f32(fast.shape[1])
    return fast * lax.rsqrt(mean + EPS) * gain


def update_kernel(at_ref, rate_ref, g0, g1, g2, g3, w_ref, q_ref, gain_ref, u_ref, out_ref, d_ref):
    head, z, y = at_ref[0], at_ref[1], at_ref[2]
    part = g0.shape[2]
    for i in range(4):
        for j in range(4):
            row = pl.multiple_of((4 * lax.rem(z + i, 4) + lax.rem(y + j, 4)) * part, 8)
            for m in range(3):
                d_ref[m, pl.ds(row, part), :] = (g0, g1, g2, g3)[i][j, m].astype(f32)
    for m in range(3):
        d = d_ref[m]
        w = w_ref[0, m].astype(f32)
        ww = w * w
        col_w = mean_of(ww, 0)
        mean_w = jnp.sum(col_w, axis=1, keepdims=True) / f32(w.shape[1])
        mean_d = jnp.sum(mean_of(d * d, 0), axis=1, keepdims=True) / f32(w.shape[1])
        factor = rate_ref[head] * jnp.sqrt((mean_w + EPS) / (mean_d + EPS))
        moved = w + factor * d
        col_m = mean_of(moved * moved, 0)
        u_ref[m] = (moved * jnp.sqrt((col_w + EPS) / (col_m + EPS))).astype(bf16)
    out_ref[...] = answer(q_ref[...], u_ref, gain_ref[...])


def update_of(at, rate, sums, weights, q, gain):
    rows, width = q.shape
    whole = lambda shape: pl.BlockSpec(shape, lambda i, at, r: (0,) * len(shape))
    shapes = [jax.ShapeDtypeStruct((3, width, width), bf16), jax.ShapeDtypeStruct((rows, width), f32)]
    return pl.pallas_call(
        update_kernel,
        out_shape=shapes,
        grid_spec=pltpu.PrefetchScalarGridSpec(
            num_scalar_prefetch=2,
            grid=(1,),
            in_specs=[
                *[whole(sums[0].shape)] * 4,
                pl.BlockSpec((1, 3, width, width), lambda i, at, r: (at[0], 0, 0, 0)),
                whole(q.shape),
                pl.BlockSpec((1, width), lambda i, at, r: (0, at[0])),
            ],
            out_specs=[whole(s.shape) for s in shapes],
            scratch_shapes=[pltpu.VMEM((3, width, width), f32)],
        ),
        compiler_params=pltpu.CompilerParams(vmem_limit_bytes=56 << 20),
        cost_estimate=pl.CostEstimate(
            flops=6 * rows * width * width, bytes_accessed=8 << 20, transcendentals=rows * width
        ),
        name="update",
    )(at, rate, *sums, weights, q, gain)


def own_kernel(at_ref, u_ref, q_ref, gain_ref, attn_ref, out_ref):
    out_ref[...] = (answer(q_ref[...], u_ref, gain_ref[...]) + attn_ref[...].astype(f32)).astype(bf16)


def own_of(at, u, queries, gain, attn):
    rows, width = attn.shape
    return pl.pallas_call(
        own_kernel,
        out_shape=jax.ShapeDtypeStruct((rows, width), bf16),
        grid_spec=pltpu.PrefetchScalarGridSpec(
            num_scalar_prefetch=1,
            grid=(1,),
            in_specs=[
                pl.BlockSpec(u.shape, lambda i, at: (0, 0, 0)),
                pl.BlockSpec((rows, width), lambda i, at: (0, at[0])),
                pl.BlockSpec((1, width), lambda i, at: (0, at[0])),
                pl.BlockSpec((rows, width), lambda i, at: (0, 0)),
            ],
            out_specs=pl.BlockSpec((rows, width), lambda i, at: (0, 0)),
        ),
        compiler_params=pltpu.CompilerParams(vmem_limit_bytes=56 << 20),
        cost_estimate=pl.CostEstimate(
            flops=6 * rows * width * width, bytes_accessed=6 << 20, transcendentals=rows * width
        ),
        name="own",
    )(at, u, queries, gain, attn)


def project_kernel(at_ref, f0, f1, f2, f3, *refs):
    lefts, rights = refs[:8], refs[8:16]
    a0, b0 = lefts[0], rights[0]
    out_ref, w_ref, f_ref, sem = refs[16:]
    z, y, core, x = at_ref[0], at_ref[1], at_ref[2], at_ref[3]
    width, cut = a0.shape[2], a0.shape[3]
    full = cut + b0.shape[3]

    def copy(src, half, g, zb, yb):
        c0 = g * full + half * cut
        row = pl.multiple_of((4 * lax.rem(zb, 2) + yb) * width, 16)
        dst = w_ref.at[pl.ds(row, width), c0 : c0 + src.shape[1]]
        return pltpu.make_async_copy(src, dst, sem.at[half, g, lax.rem(zb, 2), yb])

    for i in range(4):
        for j in range(4):
            for half, (big, small) in enumerate(((z, y), (y, z))):
                src = (lefts, rights)[half][2 * i + j // 2]
                p, q = lax.rem(big + i, 4), lax.rem(small + j, 4)
                zb, yb = (p, q) if half == 0 else (q, p)

                @pl.when(zb // 2 == core)
                def _():
                    for g in range(2):
                        copy(src.at[j % 2, g], half, g, zb, yb).start()

    for r, f in enumerate((f0, f1, f2, f3)):
        cols = pl.multiple_of(lax.rem(x + r, 4) * f.shape[1], AHD)
        f_ref[:, pl.ds(cols, f.shape[1])] = f[...]

    def arrive(zb):
        for half, src in enumerate((a0, b0)):
            for g in range(2):
                for yb in range(4):
                    copy(src.at[0, 0], half, g, zb, yb).wait()

    def tile(t, _):
        @pl.when(t == 0)
        def _():
            arrive(0)

        @pl.when(t == 2)
        def _():
            arrive(1)

        cols = pl.ds(pl.multiple_of(t * 2 * AHD, 2 * AHD), 2 * AHD)
        out_ref[:, cols] = dot(f_ref[...], w_ref[cols, :], 1, 1).astype(bf16)
        return 0

    lax.fori_loop(0, out_ref.shape[1] // (2 * AHD), tile, 0)


def project(at, fs, pieces):
    rows, full = fs[0].shape[0], 4 * fs[0].shape[1]
    width = pieces[0].shape[2]
    vmem = pl.BlockSpec(memory_space=pltpu.VMEM)
    hbm = pl.BlockSpec(memory_space=pl.ANY)
    return pl.pallas_call(
        project_kernel,
        out_shape=jax.ShapeDtypeStruct((rows, 8 * width), bf16),
        in_specs=[pl.BlockSpec(memory_space=pltpu.SMEM), *[vmem] * 4, *[hbm] * 16],
        out_specs=vmem,
        scratch_shapes=[
            pltpu.VMEM((8 * width, full), bf16),
            pltpu.VMEM((rows, full), bf16),
            pltpu.SemaphoreType.DMA((2, 2, 2, 4)),
        ],
        compiler_params=pltpu.CompilerParams(vmem_limit_bytes=40 << 20),
        cost_estimate=pl.CostEstimate(
            flops=2 * rows * full * 8 * width, bytes_accessed=10 << 20, transcendentals=0
        ),
        name="project",
    )(at, *fs, *pieces)


def scatter(chunks, axis):
    total = chunks[0].astype(f32)
    got = [hop(chunks[k], axis, k) for k in (1, 3, 2)]
    for g in got:
        total = total + g.astype(f32)
    return total.astype(bf16)


def gather(block, axis):
    got = {k: hop(block, axis, -k) for k in (1, 3, 2)}
    return [block, got[1], got[2], got[3]]


def gather_ring(parts, axis):
    low, high = jnp.stack(parts[:2]), jnp.stack(parts[2:])
    up_low, down_high = hop(low, axis, -1), hop(high, axis, 1)
    up_high, down_low = hop(high, axis, -1), hop(low, axis, 1)
    far_low, far_high = hop(up_low, axis, -1), hop(down_high, axis, 1)
    return (low, high, up_low, up_high, far_low, far_high, down_low, down_high)


def body(queries, keys, values, token_rate, head_rate, fast_weights, ttt_gain, out_weight):
    xl, z, y = lax.axis_index("xl"), lax.axis_index("z"), lax.axis_index("y")
    xh, core = lax.axis_index("xh"), lax.axis_index("core")
    x = 2 * xh + xl
    width = fast_weights.shape[2]
    at = jnp.stack([xl, z, y, x]).astype(jnp.int32)

    def cols_of(a, head):
        return lax.dynamic_slice_in_dim(a, head * width, width, 1)

    def target_of(head):
        rate = lax.dynamic_slice_in_dim(token_rate, head, 1, 1)
        return (rate * cols_of(values, head).astype(f32)).astype(bf16)

    k_got = hop(cols_of(keys, 1 - xl), "xl", 1)
    t_got = hop(target_of(1 - xl), "xl", 1)

    turned = out_weight.T
    one = along_x(turned, [(2, 0), (0, 1), (1, 2)])
    two = along_x(turned, [(2, 1), (3, 2), (1, 3)])

    packs = pack(at, queries, keys, values)
    gs = [packs[0]] + [hop(packs[k], "y", k) for k in range(1, 4)]
    parts = descent_of(at, keys, target_of(xl), k_got, t_got, fast_weights)

    low = jnp.where(x == 0, turned, jnp.where(x == 3, two, one))
    high = jnp.where(x == 3, turned, jnp.where(x == 0, one, two))
    pair = jnp.stack([low, high])
    cut = CUT * AHD
    block_a = gather(pair[:, :, :cut], "y")
    block_b = gather(pair[:, :, cut:], "z")
    queries_far = lax.optimization_barrier((queries, t_got))[0]
    q_got = hop(cols_of(queries_far, 1 - xl), "xl", 1)

    parts = scatter(parts, "z")
    pieces = (*gather_ring(block_a, "z"), *gather_ring(block_b, "y"))

    hs = [next_ring(gs[k][1:], k) for k in range(4)]

    sums = scatter(parts, "y")
    sums = gather(jnp.stack(gather(sums, "y")), "z")

    done = attend(at, gs, hs)
    backs = [done[0]] + [hop(done[k], "y", -k) for k in range(1, 4)]
    attn, other = columns_of(at, backs)
    attn_got = hop(other, "xl", 1)
    gain = ttt_gain[None, :]
    new, fast = update_of(at, head_rate, sums, fast_weights, q_got, gain)
    fast = (fast + attn_got.astype(f32)).astype(bf16)
    next_fast = along_x(fast, [(i, (i + 3) % 4) for i in range(4)])
    last_fast = along_x(fast, [(i, (i + 1) % 4) for i in range(4)])
    mine_fast = own_of(at, new, queries, gain, attn)
    far_fast = hop(mine_fast, "xh", 1)
    fs = (mine_fast, next_fast, far_fast, last_fast)

    def at_of(place):
        return jnp.stack([z, y, place, x]).astype(jnp.int32)

    sent = project(at_of(1 - core), fs, pieces)
    got = hop(sent, "core", 1)
    fs = lax.optimization_barrier((*fs, sent))[:4]
    mine = project(at_of(core), fs, pieces)
    return (mine.astype(f32) + got.astype(f32)).astype(bf16)


def solution(mesh):
    fine = Mesh(mesh.devices.reshape(2, 4, 4, 2, 2), ("xl", "z", "y", "xh", "core"))
    seq, head = ("xl", "z", "y"), ("xh", "core")
    placed = (
        P(seq, head),
        P(seq, head),
        P(seq, head),
        P(seq, head),
        P(head),
        P(head, None, None, None),
        P(head),
        P(head, seq),
    )
    return jax.shard_map(body, mesh=fine, in_specs=placed, out_specs=P(seq, head), check_vma=False)
```
